32 devices in a mesh: seq: 8 (over z, y), tp: 4 (over x, core).
Axes of the slice: x: 2, y: 2, z: 4, core: 2. Of those that a mesh axis runs over, the one named last changes fastest.
Arguments:
- tokens: bfloat16 [2048, 2560], P('seq', 'tp'), may hold values from -6 to 6
- segments: int32 [8, 256], P('seq'), may hold values from 0 to 3, never falling along the last dimension, each value on 1 to 128 neighbouring positions
- routes: int32 [2048, 6], P('seq'), may hold values from 0 to 63, all different within a row; in each aligned block of 256 rows (0 to 255, 256 to 511, ...) at most 40 rows name the same one
- page_table: int32 [8, 32], P('seq'), may hold values from 0 to 31, each once within a row
- cache_pool: bfloat16 [256, 16, 1024], P('seq', None, 'tp'), may hold values from -6 to 6
- attn_gain: float32 [2560], replicated, may hold values from 0.1 to 1.9
- w_query: bfloat16 [2560, 2048], P(None, 'tp'), may hold values from -0.125 to 0.125
- w_keyval: bfloat16 [2560, 1024], P(None, 'tp'), may hold values from -0.125 to 0.125
- w_out: bfloat16 [2048, 2560], P('tp'), may hold values from -0.125 to 0.125
- ffn_gain: float32 [2560], replicated, may hold values from 0.1 to 1.9
- w_router: bfloat16 [2560, 64], replicated, may hold values from -0.125 to 0.125
- expert_gate: bfloat16 [64, 1536, 2560], P('seq', 'tp'), may hold values from -0.125 to 0.125
- expert_up: bfloat16 [64, 1536, 2560], P('seq', 'tp'), may hold values from -0.125 to 0.125
- expert_down: bfloat16 [64, 1536, 2560], P('seq', 'tp'), may hold values from -0.15625 to 0.15625
- shared_gate: bfloat16 [1536, 2560], P('tp'), may hold values from -0.125 to 0.125
- shared_up: bfloat16 [1536, 2560], P('tp'), may hold values from -0.125 to 0.125
- shared_down: bfloat16 [1536, 2560], P('tp'), may hold values from -0.15625 to 0.15625
Outputs:
- layer_out: bfloat16 [2048, 2560], P('seq', 'tp')
- cache_out: bfloat16 [256, 16, 1024], P('seq', None, 'tp')
The draws below stay inside these ranges and needn't reach their ends.
Inputs may be any that keep to these rules, and one draw needn't show every extreme that they name: `segments`: each row is one worker's block; ids never fall along a row, every segment has 1 to 128 slots and one has exactly 128. `routes`: within the 256 tokens of one worker no expert is named more than 40 times, a bound that some block reaches. `page_table`: each row lists every page of one worker's pool once; its first 16 entries take the worker's blocks in order.
All inputs are finite; a program needn't handle non-finite values.
Results may differ from the reference program's by a relative error of at most 0.019.
Values may be sent and summed in bfloat16 or wider, within the bound.
A program may use at most 192 MiB of HBM per device.

```python
import math
import jax
import jax.numpy as jnp
import numpy as np
from jax import lax

D = 2560
Q_HEADS = 16
KV_HEADS = 4
HEAD = 128
EXPERTS = 64
TOP = 6
MOE_FF = 1536
SHARED_FF = 1536
PAGE = 16
REQ_DEV = 4
TOK_DEV = 256
WORKERS = 8
TOKENS = 2048
MAX_LEN = 128
CAP = 40
HID_GROUPS = 4
CACHE_W = 1024
PAGES_DEV = 16
POOL_DEV = 32
POOL = 256


def block_scale(rng, dims, pieces, least, largest):
    loudness = 1.0
    for dim, parts in pieces:
        heights = jax.random.uniform(jax.random.fold_in(jax.random.fold_in(rng, 6), dim), (parts,), jnp.float32, least / len(pieces), largest / len(pieces))
        loudness = loudness * jnp.repeat(jnp.exp(heights), dims[dim] // parts).reshape((-1,) + (1,) * (len(dims) - 1 - dim))
    return loudness


def length_profile(number_of, total, bound, slope):
    weights = [(1 << 20) // math.isqrt(standing ** slope) + 1 for standing in range(2, number_of + 1)]
    rest, holding = total - bound - (number_of - 1), [1] * (number_of - 1)
    while rest > 0:
        candidates = [i for i in range(number_of - 1) if holding[i] < bound]
        whole, budget = sum([weights[i] for i in candidates]), rest
        for i in candidates:
            more = min(bound - holding[i], max(1, budget * weights[i] // whole), rest)
            holding[i] = holding[i] + more
            rest = rest - more
    return np.array([bound] + holding)


def ragged(rng, amount, total, limit, lean):
    if amount == 2:
        one = jax.random.randint(rng, (), max(1, total - limit), min(limit, total - 1) + 1)
        return jnp.stack([one, total - one])
    lengths = jnp.asarray(length_profile(amount, total, limit, lean), jnp.int32)
    couples = (amount - 1) // 2
    giver, sink = lengths[1:1 + 2 * couples:2], lengths[2:2 + 2 * couples:2]
    slack = jnp.minimum(giver - 1, limit - sink)
    moved = jax.random.randint(jax.random.fold_in(rng, 1), (couples,), 0, 1 << 20) % (slack + 1)
    lengths = lengths.at[1:1 + 2 * couples:2].set(giver - moved).at[2:2 + 2 * couples:2].set(sink + moved)
    return lengths[jax.random.permutation(jax.random.fold_in(rng, 2), amount)]


def deal_out(rng, own, number, rows, count, top, most, lean):
    order = jax.random.permutation(rng, count)
    heavy_load, common = load_shares(count, rows * top, most, lean, True), load_shares(count, rows * top, most, lean, False)
    places = jnp.arange(count)

    def named(tallies, offset_by):
        used = int((tallies > 0).sum())
        fixed = max(1, used // 4)
        passed = fixed + (places - fixed + offset_by * (used - fixed)) % max(1, count - fixed)
        return jnp.zeros((count,), jnp.int32).at[order[jnp.where(places < fixed, places, passed)]].set(jnp.asarray(tallies, jnp.int32))

    tallies = jnp.where(number % 4 == 0, named(heavy_load, number // 4), named(common, number - number // 4 - 1))
    mixed = jax.random.permutation(jax.random.fold_in(own, 3), count)
    source_of, sink = mixed[0:count // 2 * 2:2], mixed[1:count // 2 * 2:2]
    slack = jnp.minimum(tallies[source_of] - 1, most - tallies[sink]) // 2
    slack = jnp.where((source_of == order[0]) | (sink == order[0]) | (tallies[sink] == 0), 0, jnp.maximum(slack, 0))
    passed = jax.random.randint(jax.random.fold_in(own, 4), (count // 2,), 0, 1 << 20) % (slack + 1)
    tallies = tallies.at[source_of].add(-passed).at[sink].add(passed)
    members = jnp.searchsorted(jnp.cumsum(tallies), jnp.arange(rows * top), side="right").astype(jnp.int32)
    grid = members.reshape(top, rows).T
    grid = grid[jax.random.permutation(jax.random.fold_in(own, 1), rows)]
    offset_by = jax.random.randint(jax.random.fold_in(own, 2), (rows, 1), 0, top)
    return jnp.take_along_axis(grid, (jnp.arange(top)[None, :] + offset_by) % top, axis=1)


def load_shares(count, total, limit, lean, full):
    portions = [(1 << 20) // math.isqrt(rank ** lean) + 1 for rank in range(1, count + 1)]
    largest = limit if full else min(limit, max(-(-total // count), total * portions[0] // sum(portions)))
    least = 1 if total - largest >= count - 1 else 0
    given, rest = [largest] + [least] * (count - 1), total - largest - least * (count - 1)
    while rest > 0:
        candidates = [i for i in range(1, count) if given[i] < largest] or [i for i in range(1, count) if given[i] < limit]
        pool, left = sum([portions[i] for i in candidates]), rest
        for i in candidates:
            extra = min(limit - given[i], max(1, left * portions[i] // pool), rest)
            given[i] = given[i] + extra
            rest = rest - extra
    return np.array(given)


def scatter_about(own_key, extent, spread, limit, pieces=(), held_as=jnp.bfloat16):
    factor_of = block_scale(own_key, extent, pieces, -0.22, 0.18) if pieces else 1.0
    drawn = jax.random.normal(own_key, extent, jnp.float32) * spread * factor_of
    return jnp.minimum(jnp.maximum(drawn, -limit), limit).astype(held_as)


def setup_inputs(seed: int = 0) -> dict:
    splits = jax.random.split(jax.random.key(seed), 18)
    tokens = scatter_about(splits[0], (TOKENS, D), 1.0, 6.0, ((0, 8), (1, 4)))
    segments = jax.vmap(lambda own: jnp.searchsorted(jnp.cumsum(ragged(own, REQ_DEV, TOK_DEV, MAX_LEN, 2)), jnp.arange(TOK_DEV), side="right"))(jax.random.split(splits[1], WORKERS)).reshape((WORKERS, TOK_DEV)).astype(jnp.int32)
    routes_keys = jax.random.split(jax.random.fold_in(splits[2], 1), TOKENS // TOK_DEV)
    routes_turns = jax.random.permutation(jax.random.fold_in(splits[2], 3), TOKENS // TOK_DEV)
    routes = jax.vmap(lambda own, number: deal_out(jax.random.fold_in(splits[2], 2), own, number, TOK_DEV, EXPERTS, TOP, CAP, 2))(routes_keys, routes_turns).reshape((TOKENS, TOP))
    page_table = jax.vmap(lambda own: jax.random.permutation(own, POOL_DEV))(jax.random.split(splits[3], WORKERS)).reshape((WORKERS, POOL_DEV)).astype(jnp.int32)
    cache_pool = scatter_about(splits[4], (POOL, PAGE, CACHE_W), 1.0, 6.0, ((0, 8), (2, 4)))
    attn_gain = jnp.clip(1.0 + 0.18 * jax.random.normal(splits[5], (D,), jnp.float32), 0.1, 1.9)
    w_query = scatter_about(splits[6], (D, Q_HEADS * HEAD), D ** -0.5, 0.125, ((1, 4),))
    w_keyval = scatter_about(splits[7], (D, CACHE_W), D ** -0.5, 0.125, ((1, 4),))
    w_out = scatter_about(splits[8], (Q_HEADS * HEAD, D), (Q_HEADS * HEAD) ** -0.5, 0.125, ((0, 4),))
    ffn_gain = jnp.clip(1.0 + 0.18 * jax.random.normal(splits[9], (D,), jnp.float32), 0.1, 1.9)
    w_router = scatter_about(splits[10], (D, EXPERTS), D ** -0.5, 0.125)
    expert_gate = scatter_about(splits[11], (EXPERTS, MOE_FF, D), D ** -0.5, 0.125, ((0, 8), (1, 4)))
    expert_up = scatter_about(splits[12], (EXPERTS, MOE_FF, D), D ** -0.5, 0.125, ((0, 8), (1, 4)))
    expert_down = scatter_about(splits[13], (EXPERTS, MOE_FF, D), MOE_FF ** -0.5, 0.15625, ((0, 8), (1, 4)))
    shared_gate = scatter_about(splits[14], (SHARED_FF, D), D ** -0.5, 0.125, ((0, 4),))
    shared_up = scatter_about(splits[15], (SHARED_FF, D), D ** -0.5, 0.125, ((0, 4),))
    shared_down = scatter_about(splits[16], (SHARED_FF, D), SHARED_FF ** -0.5, 0.15625, ((0, 4),))
    return {"tokens": tokens, "segments": segments, "routes": routes, "page_table": page_table, "cache_pool": cache_pool, "attn_gain": attn_gain, "w_query": w_query, "w_keyval": w_keyval, "w_out": w_out, "ffn_gain": ffn_gain, "w_router": w_router, "expert_gate": expert_gate, "expert_up": expert_up, "expert_down": expert_down, "shared_gate": shared_gate, "shared_up": shared_up, "shared_down": shared_down}


norm_eps = 1e-05
rope_base = 500000.0

def rms_scale(inputs, gain_vec):
    return inputs * lax.rsqrt(lax.optimization_barrier(jnp.mean(inputs * inputs, axis=-1, keepdims=True)) + norm_eps) * gain_vec

def in_segment(segment_row):
    row_count = segment_row.shape[0]
    row_order = jnp.arange(row_count, dtype=jnp.int32)
    earlier = jnp.concatenate([segment_row[:1] - 1, segment_row[:-1]])
    starts = jnp.where(segment_row != earlier, row_order, 0)
    return row_order - lax.cummax(starts, axis=0)

def rotate(inputs, position):
    half_size = inputs.shape[-1] // 2
    inv_freq = rope_base ** (-jnp.arange(half_size, dtype=jnp.float32) * 2.0 / inputs.shape[-1])
    angles = position.astype(jnp.float32)[:, None] * inv_freq[None, :]
    cosine = jnp.cos(angles)[:, None, :]
    sine_term = jnp.sin(angles)[:, None, :]
    leading = inputs[..., :half_size]
    trailing = inputs[..., half_size:]
    return jnp.concatenate([leading * cosine - trailing * sine_term, trailing * cosine + leading * sine_term], axis=-1)

def reference(tokens, segments, routes, page_table, cache_pool, attn_gain, w_query, w_keyval, w_out, ffn_gain, w_router, expert_gate, expert_up, expert_down, shared_gate, shared_up, shared_down):

    def attend_worker(inputs):
        block_rows, segment_row = inputs
        row_count = block_rows.shape[0]
        normed_in = rms_scale(block_rows.astype(jnp.float32), attn_gain).astype(jnp.bfloat16)
        position = in_segment(segment_row)
        queries = jnp.dot(normed_in, w_query, preferred_element_type=jnp.float32).reshape(row_count, Q_HEADS, HEAD)
        queries = rotate(queries, position).astype(jnp.bfloat16)
        keyval = jnp.dot(normed_in, w_keyval, preferred_element_type=jnp.float32).reshape(row_count, KV_HEADS, 2, HEAD)
        key_rows = rotate(keyval[:, :, 0], position).astype(jnp.bfloat16)
        values = keyval[:, :, 1].astype(jnp.bfloat16)
        new_cache = jnp.stack([key_rows, values], axis=2).reshape(row_count, CACHE_W)
        grouped = queries.reshape(row_count, KV_HEADS, Q_HEADS // KV_HEADS, HEAD)
        scores = jnp.einsum('qgjd,kgd->gjqk', grouped.astype(jnp.float32), key_rows.astype(jnp.float32)) * HEAD ** (-0.5)
        row_order = jnp.arange(row_count, dtype=jnp.int32)
        allowed = (segment_row[:, None] == segment_row[None, :]) & (row_order[None, :] <= row_order[:, None])
        weights = jnp.where(allowed, jnp.exp(scores), 0.0)
        attn_probs = (weights / lax.optimization_barrier(jnp.sum(weights, axis=-1, keepdims=True))).astype(jnp.bfloat16)
        attended = jnp.einsum('gjqk,kgd->qgjd', attn_probs.astype(jnp.float32), values.astype(jnp.float32))
        attended = attended.astype(jnp.bfloat16).reshape(row_count, Q_HEADS * HEAD)
        hidden_state = block_rows.astype(jnp.float32) + jnp.dot(attended, w_out, preferred_element_type=jnp.float32)
        return (hidden_state, new_cache)
    hidden_state, new_cache = lax.map(attend_worker, (tokens.reshape(WORKERS, TOK_DEV, D), segments))
    hidden_flat = hidden_state.reshape(TOKENS, D)
    normed_mid = rms_scale(hidden_flat, ffn_gain).astype(jnp.bfloat16)
    logits = jnp.dot(normed_mid, w_router, preferred_element_type=jnp.float32)
    lifted = jnp.exp(jnp.take_along_axis(logits, routes, axis=1))
    route_weight = lifted / lax.optimization_barrier(jnp.sum(lifted, axis=1, keepdims=True))
    shared_act = (jax.nn.silu(jnp.dot(normed_mid, shared_gate.T, preferred_element_type=jnp.float32)) * jnp.dot(normed_mid, shared_up.T, preferred_element_type=jnp.float32)).astype(jnp.bfloat16)
    shared_out = jnp.dot(shared_act, shared_down, preferred_element_type=jnp.float32)
    flat_routes = routes.reshape(WORKERS, TOK_DEV * TOP)
    onehot = (flat_routes[:, :, None] == jnp.arange(EXPERTS, dtype=jnp.int32)[None, None, :]).astype(jnp.int32)
    slot_rank = lax.optimization_barrier(jnp.sum((jnp.cumsum(onehot, axis=1) - onehot) * onehot, axis=2))
    worker_ids = jnp.arange(WORKERS, dtype=jnp.int32)[:, None]
    slot_index = (flat_routes * (WORKERS * CAP) + worker_ids * CAP + slot_rank).reshape(-1)
    token_ids = jnp.arange(TOKENS * TOP, dtype=jnp.int32) // TOP
    slot_owner = jnp.full((EXPERTS * WORKERS * CAP,), TOKENS, jnp.int32).at[slot_index].set(token_ids)
    padded = jnp.concatenate([normed_mid, jnp.zeros((1, D), normed_mid.dtype)], axis=0)
    dispatch = padded[slot_owner].reshape(EXPERTS, WORKERS * CAP, D)

    def run_expert(inputs):
        slot_rows, gate_w, up_w, down_w = inputs
        activation = (jax.nn.silu(jnp.dot(slot_rows, gate_w.T, preferred_element_type=jnp.float32)) * jnp.dot(slot_rows, up_w.T, preferred_element_type=jnp.float32)).astype(jnp.bfloat16)
        group_width = MOE_FF // HID_GROUPS
        running = jnp.zeros((slot_rows.shape[0], D), jnp.float32)
        for group_id in range(HID_GROUPS):
            part_sum = jnp.dot(activation[:, group_id * group_width:(group_id + 1) * group_width], down_w[group_id * group_width:(group_id + 1) * group_width], preferred_element_type=jnp.float32)
            running = running + lax.optimization_barrier(part_sum.astype(jnp.bfloat16)).astype(jnp.float32)
        return running
    expert_out = lax.map(run_expert, (dispatch, expert_gate, expert_up, expert_down))
    gathered = expert_out.reshape(EXPERTS * WORKERS * CAP, D)[slot_index].reshape(TOKENS, TOP, D)
    routed = lax.optimization_barrier(jnp.sum(route_weight[:, :, None] * gathered, axis=1))
    layer_out = (hidden_flat + shared_out + routed).astype(jnp.bfloat16)
    pool_rows = cache_pool.reshape(WORKERS, POOL_DEV, PAGE, CACHE_W)
    new_pages = new_cache.reshape(WORKERS, PAGES_DEV, PAGE, CACHE_W)

    def write_pages(inputs):
        worker_pool, table_row, worker_pages = inputs
        return worker_pool.at[table_row[:PAGES_DEV]].set(worker_pages)
    cache_out = lax.map(write_pages, (pool_rows, page_table, new_pages)).reshape(POOL, PAGE, CACHE_W)
    return (layer_out, cache_out)
```

```python
import jax
import jax.numpy as jnp
from jax import lax
from jax.sharding import PartitionSpec as P

HEAD = 128
PAGE = 16


norm_eps = 1e-05
rope_base = 500000.0


def partner(block, axis, distance):
    count = lax.axis_size(axis)
    route = []
    for low in range(count):
        high = low | 1 << distance
        if high != low and high < count:
            route += [(low, high), (high, low)]
    return lax.ppermute(block, axis, route)


def gather_all(block):
    return lax.all_gather(block, ("seq", "tp"), axis=0)


def scatter_all(whole):
    part = lax.psum_scatter(whole, "tp", scatter_dimension=2, tiled=True)
    return lax.psum_scatter(part, "seq", scatter_dimension=0, tiled=False)


def rms_scale(inputs, gain_vec):
    return (
        inputs * lax.rsqrt(jnp.mean(inputs * inputs, axis=-1, keepdims=True) + norm_eps) * gain_vec
    )


def in_segment(segment_row):
    row_order = jnp.arange(segment_row.shape[0], dtype=jnp.int32)
    before = (segment_row[:, None] == segment_row[None, :]) & (
        row_order[None, :] < row_order[:, None]
    )
    return jnp.sum(before.astype(jnp.int32), axis=1)


def rotate(inputs, position):
    half_size = inputs.shape[-1] // 2
    inv_freq = rope_base ** (-jnp.arange(half_size, dtype=jnp.float32) * 2.0 / inputs.shape[-1])
    angles = position.astype(jnp.float32)[:, None] * inv_freq[None, :]
    cosine = jnp.cos(angles)[:, None, :]
    sine_term = jnp.sin(angles)[:, None, :]
    leading = inputs[..., :half_size]
    trailing = inputs[..., half_size:]
    return jnp.concatenate(
        [leading * cosine - trailing * sine_term, trailing * cosine + leading * sine_term], axis=-1
    )


def shards(
    tokens,
    segments,
    routes,
    page_table,
    cache_pool,
    attn_gain,
    w_query,
    w_keyval,
    w_out,
    ffn_gain,
    w_router,
    expert_gate,
    expert_up,
    expert_down,
    shared_gate,
    shared_up,
    shared_down,
):
    tp_count = lax.axis_size("tp")
    seq_count = lax.axis_size("seq")
    tp_rank = lax.axis_index("tp")
    row_count = tokens.shape[0]
    col_width = tokens.shape[1]
    model_width = col_width * tp_count
    whole_rows = lax.all_gather(tokens, "tp", axis=1, tiled=True)
    residual = whole_rows.astype(jnp.float32)
    normed_in = rms_scale(residual, attn_gain).astype(jnp.bfloat16)
    segment_row = segments[0]
    position = in_segment(segment_row)
    local_heads = w_query.shape[1] // HEAD
    queries = jnp.dot(normed_in, w_query, preferred_element_type=jnp.float32).reshape(
        row_count, local_heads, HEAD
    )
    queries = rotate(queries, position).astype(jnp.bfloat16)
    keyval = jnp.dot(normed_in, w_keyval, preferred_element_type=jnp.float32)
    if w_keyval.shape[1] == HEAD:
        is_key = tp_rank % 2 == 0
        rotated = rotate(keyval.reshape(row_count, 1, HEAD), position).reshape(row_count, HEAD)
        own_half = jnp.where(is_key, rotated, keyval).astype(jnp.bfloat16)
        other_half = partner(own_half, "tp", 0)
        key_rows = jnp.where(is_key, own_half, other_half)
        values = jnp.where(is_key, other_half, own_half)
        cache_rows = own_half
    else:
        key_rows = (
            rotate(keyval[:, :HEAD].reshape(row_count, 1, HEAD), position)
            .reshape(row_count, HEAD)
            .astype(jnp.bfloat16)
        )
        values = keyval[:, HEAD:].astype(jnp.bfloat16)
        cache_rows = jnp.concatenate([key_rows, values], axis=1)
    scores = jnp.einsum(
        "qhd,kd->hqk", queries, key_rows, preferred_element_type=jnp.float32
    ) * HEAD ** (-0.5)
    row_order = jnp.arange(row_count, dtype=jnp.int32)
    allowed = (segment_row[:, None] == segment_row[None, :]) & (
        row_order[None, :] <= row_order[:, None]
    )
    weights = jnp.where(allowed[None], jnp.exp(scores), 0.0)
    attn_probs = (weights / jnp.sum(weights, axis=-1, keepdims=True)).astype(jnp.bfloat16)
    attended = jnp.einsum("hqk,kd->qhd", attn_probs, values, preferred_element_type=jnp.float32)
    attended = attended.astype(jnp.bfloat16).reshape(row_count, local_heads * HEAD)
    attn_part = jnp.dot(attended, w_out, preferred_element_type=jnp.float32)
    attn_mine = lax.psum_scatter(
        attn_part.astype(jnp.bfloat16), "tp", scatter_dimension=1, tiled=True
    )
    hidden_mine = tokens.astype(jnp.float32) + attn_mine.astype(jnp.float32)
    seq_rank = lax.axis_index("seq")
    gathered = gather_all(hidden_mine.astype(jnp.bfloat16))
    hidden_all = (
        gathered.reshape(seq_count, tp_count, row_count, col_width)
        .transpose(0, 2, 1, 3)
        .reshape(seq_count, row_count, model_width)
    )
    normed_all = rms_scale(hidden_all.astype(jnp.float32), ffn_gain).astype(jnp.bfloat16)

    top_count = routes.shape[1]
    local_experts = expert_gate.shape[0]
    expert_total = local_experts * seq_count
    capacity = (
        (row_count * top_count * 5 // (expert_total * 3) + tp_count - 1) // tp_count * tp_count
    )
    slots = local_experts * capacity
    routes_all = lax.all_gather(routes, "seq", axis=0)
    chosen = jnp.sum(
        (routes_all[:, :, :, None] == jnp.arange(expert_total, dtype=jnp.int32)).astype(
            jnp.float32
        ),
        axis=2,
    )
    logits = jnp.einsum("wtd,de->wte", normed_all, w_router, preferred_element_type=jnp.float32)
    lifted = jnp.where(chosen > 0, jnp.exp(logits), 0.0)
    route_weight = lifted / jnp.sum(lifted, axis=2, keepdims=True)
    first = seq_rank * local_experts
    named = lax.dynamic_slice_in_dim(chosen, first, local_experts, 2)
    weight_mine = lax.dynamic_slice_in_dim(route_weight, first, local_experts, 2)
    earlier = (row_order[:, None] > row_order[None, :]).astype(jnp.bfloat16)
    rank = jnp.einsum(
        "ts,wse->wte", earlier, named.astype(jnp.bfloat16), preferred_element_type=jnp.float32
    ).astype(jnp.int32)
    place = jnp.where(named > 0, rank, -1)
    hit = place.transpose(0, 2, 1)[:, :, None, :] == jnp.arange(capacity, dtype=jnp.int32)[
        None, None, :, None
    ]
    select = hit.astype(jnp.bfloat16).reshape(seq_count, slots, row_count)
    slot_weight = jnp.sum(
        jnp.where(hit, weight_mine.transpose(0, 2, 1)[:, :, None, :], 0.0), axis=3
    )
    slot_rows = jnp.einsum(
        "wst,wtd->wsd", select, normed_all, preferred_element_type=jnp.float32
    ).astype(jnp.bfloat16).reshape(seq_count, local_experts, capacity, model_width)
    gate_out = jnp.einsum(
        "secd,efd->secf", slot_rows, expert_gate, preferred_element_type=jnp.float32
    )
    up_out = jnp.einsum("secd,efd->secf", slot_rows, expert_up, preferred_element_type=jnp.float32)
    activation = (jax.nn.silu(gate_out) * up_out * slot_weight[..., None]).astype(jnp.bfloat16)
    group_part = jnp.einsum(
        "secf,efd->secd", activation, expert_down, preferred_element_type=jnp.float32
    ).astype(jnp.bfloat16).reshape(seq_count, slots, model_width)
    normed_mid = lax.dynamic_index_in_dim(normed_all, seq_rank, 0, keepdims=False)
    shared_gate_out = jnp.einsum(
        "td,fd->tf", normed_mid, shared_gate, preferred_element_type=jnp.float32
    )
    shared_up_out = jnp.einsum(
        "td,fd->tf", normed_mid, shared_up, preferred_element_type=jnp.float32
    )
    shared_act = (jax.nn.silu(shared_gate_out) * shared_up_out).astype(jnp.bfloat16)
    shared_part = jnp.dot(shared_act, shared_down, preferred_element_type=jnp.float32)
    routed_part = jnp.einsum(
        "wst,wsd->wtd", select, group_part, preferred_element_type=jnp.float32
    )
    is_mine = jnp.arange(seq_count, dtype=jnp.int32)[:, None, None] == seq_rank
    summand = routed_part + jnp.where(is_mine, shared_part[None], 0.0)
    output_share = scatter_all(summand.astype(jnp.bfloat16)).astype(jnp.float32)
    layer_out = (hidden_mine + output_share).astype(jnp.bfloat16)
    page_count = row_count // PAGE
    new_pages = cache_rows.reshape(page_count, PAGE, cache_rows.shape[1])
    cache_out = cache_pool.at[page_table[0, :page_count]].set(new_pages)
    return (layer_out, cache_out)


def solution(mesh):
    in_specs = (
        P("seq", "tp"),
        P("seq", None),
        P("seq", None),
        P("seq", None),
        P("seq", None, "tp"),
        P(),
        P(None, "tp"),
        P(None, "tp"),
        P("tp", None),
        P(),
        P(),
        P("seq", "tp", None),
        P("seq", "tp", None),
        P("seq", "tp", None),
        P("tp", None),
        P("tp", None),
        P("tp", None),
    )
    out_specs = (P("seq", "tp"), P("seq", None, "tp"))
    return jax.shard_map(shards, mesh=mesh, in_specs=in_specs, out_specs=out_specs, check_vma=False)
```

```python
import jax
import jax.numpy as jnp
from jax import lax
from jax.experimental import pallas as pl
from jax.experimental.pallas import tpu as pltpu
from jax.sharding import PartitionSpec as P

HEAD = 128
PAGE = 16


norm_eps = 1e-05
rope_base = 500000.0


def partner(block, axis, distance):
    count = lax.axis_size(axis)
    route = []
    for low in range(count):
        high = low | 1 << distance
        if high != low and high < count:
            route += [(low, high), (high, low)]
    return lax.ppermute(block, axis, route)


def gather_all(block):
    return lax.all_gather(block, ("seq", "tp"), axis=0)


def scatter_all(whole):
    part = lax.psum_scatter(whole, "tp", scatter_dimension=0, tiled=False)
    return lax.psum_scatter(part, "seq", scatter_dimension=0, tiled=False)


def dispatch_body(rows_ref, select_ref, gain_ref, router_ref, slot_ref, logit_ref):
    parts, _, width = rows_ref.shape
    total = None
    for part in range(parts):
        block = rows_ref[part].astype(jnp.float32)
        square = jnp.sum(block * block, axis=1, keepdims=True)
        total = square if total is None else total + square
    scale = lax.rsqrt(total / (parts * width) + norm_eps)
    select = select_ref[...]
    logit = None
    for part in range(parts):
        columns = slice(part * width, (part + 1) * width)
        normed = (
            rows_ref[part].astype(jnp.float32) * scale * gain_ref[:, columns]
        ).astype(jnp.bfloat16)
        slot_ref[:, columns] = jnp.dot(
            select, normed, preferred_element_type=jnp.float32
        ).astype(jnp.bfloat16)
        term = jnp.dot(normed, router_ref[columns, :], preferred_element_type=jnp.float32)
        logit = term if logit is None else logit + term
    logit_ref[...] = logit


def dispatch(gathered, select, gain, router):
    workers, parts, rows, width = gathered.shape
    slots = select.shape[1]
    model_width = parts * width
    return pl.pallas_call(
        dispatch_body,
        grid=(workers,),
        in_specs=[
            pl.BlockSpec((None, parts, rows, width), lambda w: (w, 0, 0, 0)),
            pl.BlockSpec((None, slots, rows), lambda w: (w, 0, 0)),
            pl.BlockSpec((1, model_width), lambda w: (0, 0)),
            pl.BlockSpec((model_width, router.shape[1]), lambda w: (0, 0)),
        ],
        out_specs=[
            pl.BlockSpec((None, slots, model_width), lambda w: (w, 0, 0)),
            pl.BlockSpec((None, rows, router.shape[1]), lambda w: (w, 0, 0)),
        ],
        out_shape=[
            jax.ShapeDtypeStruct((workers, slots, model_width), jnp.bfloat16),
            jax.ShapeDtypeStruct((workers, rows, router.shape[1]), jnp.float32),
        ],
        compiler_params=pltpu.CompilerParams(vmem_limit_bytes=32 << 20),
    )(gathered, select, gain[None, :], router)


def combine_body(parts, place_ref, expert_ref, shared_ref, out_ref):
    width = out_ref.shape[2]
    place = place_ref[...]
    is_mine = pl.program_id(0) == lax.axis_index("seq")
    for part in range(parts):
        columns = slice(part * width, (part + 1) * width)
        routed = jnp.dot(place, expert_ref[:, columns], preferred_element_type=jnp.float32)
        out_ref[part] = (routed + jnp.where(is_mine, shared_ref[:, columns], 0.0)).astype(
            jnp.bfloat16
        )


def combine(place, expert_rows, shared_part, parts):
    workers, rows, slots = place.shape
    model_width = expert_rows.shape[2]
    width = model_width // parts
    return pl.pallas_call(
        lambda *refs: combine_body(parts, *refs),
        grid=(workers,),
        in_specs=[
            pl.BlockSpec((None, rows, slots), lambda w: (w, 0, 0)),
            pl.BlockSpec((None, slots, model_width), lambda w: (w, 0, 0)),
            pl.BlockSpec((rows, model_width), lambda w: (0, 0)),
        ],
        out_specs=pl.BlockSpec((parts, None, rows, width), lambda w: (0, w, 0, 0)),
        out_shape=jax.ShapeDtypeStruct((parts, workers, rows, width), jnp.bfloat16),
        compiler_params=pltpu.CompilerParams(vmem_limit_bytes=32 << 20),
    )(place, expert_rows, shared_part)


def rms_scale(inputs, gain_vec):
    return (
        inputs * lax.rsqrt(jnp.mean(inputs * inputs, axis=-1, keepdims=True) + norm_eps) * gain_vec
    )


def in_segment(segment_row):
    row_order = jnp.arange(segment_row.shape[0], dtype=jnp.int32)
    before = (segment_row[:, None] == segment_row[None, :]) & (
        row_order[None, :] < row_order[:, None]
    )
    return jnp.sum(before.astype(jnp.int32), axis=1)


def rotate(inputs, position):
    half_size = inputs.shape[-1] // 2
    inv_freq = rope_base ** (-jnp.arange(half_size, dtype=jnp.float32) * 2.0 / inputs.shape[-1])
    angles = position.astype(jnp.float32)[:, None] * inv_freq[None, :]
    cosine = jnp.cos(angles)[:, None, :]
    sine_term = jnp.sin(angles)[:, None, :]
    leading = inputs[..., :half_size]
    trailing = inputs[..., half_size:]
    return jnp.concatenate(
        [leading * cosine - trailing * sine_term, trailing * cosine + leading * sine_term], axis=-1
    )


def shards(
    tokens,
    segments,
    routes,
    page_table,
    cache_pool,
    attn_gain,
    w_query,
    w_keyval,
    w_out,
    ffn_gain,
    w_router,
    expert_gate,
    expert_up,
    expert_down,
    shared_gate,
    shared_up,
    shared_down,
):
    tp_count = lax.axis_size("tp")
    seq_count = lax.axis_size("seq")
    tp_rank = lax.axis_index("tp")
    row_count = tokens.shape[0]
    col_width = tokens.shape[1]
    model_width = col_width * tp_count
    whole_rows = lax.all_gather(tokens, "tp", axis=1, tiled=True)
    residual = whole_rows.astype(jnp.float32)
    normed_in = rms_scale(residual, attn_gain).astype(jnp.bfloat16)
    segment_row = segments[0]
    position = in_segment(segment_row)
    local_heads = w_query.shape[1] // HEAD
    queries = jnp.dot(normed_in, w_query, preferred_element_type=jnp.float32).reshape(
        row_count, local_heads, HEAD
    )
    queries = rotate(queries, position).astype(jnp.bfloat16)
    keyval = jnp.dot(normed_in, w_keyval, preferred_element_type=jnp.float32)
    if w_keyval.shape[1] == HEAD:
        is_key = tp_rank % 2 == 0
        rotated = rotate(keyval.reshape(row_count, 1, HEAD), position).reshape(row_count, HEAD)
        own_half = jnp.where(is_key, rotated, keyval).astype(jnp.bfloat16)
        other_half = partner(own_half, "tp", 0)
        key_rows = jnp.where(is_key, own_half, other_half)
        values = jnp.where(is_key, other_half, own_half)
        cache_rows = own_half
    else:
        key_rows = (
            rotate(keyval[:, :HEAD].reshape(row_count, 1, HEAD), position)
            .reshape(row_count, HEAD)
            .astype(jnp.bfloat16)
        )
        values = keyval[:, HEAD:].astype(jnp.bfloat16)
        cache_rows = jnp.concatenate([key_rows, values], axis=1)
    scores = jnp.einsum(
        "qhd,kd->hqk", queries, key_rows, preferred_element_type=jnp.float32
    ) * HEAD ** (-0.5)
    row_order = jnp.arange(row_count, dtype=jnp.int32)
    allowed = (segment_row[:, None] == segment_row[None, :]) & (
        row_order[None, :] <= row_order[:, None]
    )
    weights = jnp.where(allowed[None], jnp.exp(scores), 0.0)
    attn_probs = (weights / jnp.sum(weights, axis=-1, keepdims=True)).astype(jnp.bfloat16)
    attended = jnp.einsum("hqk,kd->qhd", attn_probs, values, preferred_element_type=jnp.float32)
    attended = attended.astype(jnp.bfloat16).reshape(row_count, local_heads * HEAD)
    attn_part = jnp.dot(attended, w_out, preferred_element_type=jnp.float32)
    attn_mine = lax.psum_scatter(
        attn_part.astype(jnp.bfloat16)
        .reshape(row_count, tp_count, col_width)
        .transpose(1, 0, 2),
        "tp",
        scatter_dimension=0,
        tiled=False,
    )
    hidden_mine = tokens.astype(jnp.float32) + attn_mine.astype(jnp.float32)
    seq_rank = lax.axis_index("seq")
    gathered = gather_all(hidden_mine.astype(jnp.bfloat16))
    gathered = gathered.reshape(seq_count, tp_count, row_count, col_width)

    top_count = routes.shape[1]
    local_experts = expert_gate.shape[0]
    expert_total = local_experts * seq_count
    capacity = (
        (row_count * top_count * 5 // (expert_total * 3) + tp_count - 1) // tp_count * tp_count
    )
    capacity = (capacity + 15) // 16 * 16
    slots = local_experts * capacity
    marks = jnp.sum(
        (routes[:, :, None] == jnp.arange(expert_total, dtype=jnp.int32)).astype(jnp.float32),
        axis=1,
    ).astype(jnp.bfloat16)
    marks = jnp.pad(marks, ((0, 0), (0, -expert_total % 128)))
    chosen = lax.all_gather(marks, "seq", axis=0)[:, :, :expert_total].astype(jnp.float32)
    first = seq_rank * local_experts
    named = lax.dynamic_slice_in_dim(chosen, first, local_experts, 2)
    earlier = (row_order[:, None] > row_order[None, :]).astype(jnp.bfloat16)
    rank = jnp.einsum(
        "ts,wse->wte", earlier, named.astype(jnp.bfloat16), preferred_element_type=jnp.float32
    ).astype(jnp.int32)
    place = jnp.where(named > 0, rank, -1)
    hit = place.transpose(0, 2, 1)[:, :, None, :] == jnp.arange(capacity, dtype=jnp.int32)[
        None, None, :, None
    ]
    select = hit.astype(jnp.bfloat16).reshape(seq_count, slots, row_count)
    place_back = (
        place[:, :, :, None] == jnp.arange(capacity, dtype=jnp.int32)[None, None, None, :]
    ).astype(jnp.bfloat16).reshape(seq_count, row_count, slots)
    slot_rows, logits = dispatch(gathered, select, ffn_gain, w_router)
    slot_rows = slot_rows.reshape(seq_count, local_experts, capacity, model_width)
    lifted = jnp.where(chosen > 0, jnp.exp(logits), 0.0)
    route_weight = lifted / jnp.sum(lifted, axis=2, keepdims=True)
    weight_mine = lax.dynamic_slice_in_dim(route_weight, first, local_experts, 2)
    slot_weight = jnp.sum(
        jnp.where(hit, weight_mine.transpose(0, 2, 1)[:, :, None, :], 0.0), axis=3
    )
    gate_out = jnp.einsum(
        "secd,efd->secf", slot_rows, expert_gate, preferred_element_type=jnp.float32
    )
    up_out = jnp.einsum("secd,efd->secf", slot_rows, expert_up, preferred_element_type=jnp.float32)
    activation = (jax.nn.silu(gate_out) * up_out * slot_weight[..., None]).astype(jnp.bfloat16)
    group_part = jnp.einsum(
        "secf,efd->secd", activation, expert_down, preferred_element_type=jnp.float32
    ).astype(jnp.bfloat16).reshape(seq_count, slots, model_width)
    own_rows = lax.dynamic_index_in_dim(gathered, seq_rank, 0, keepdims=False)
    own_rows = own_rows.transpose(1, 0, 2).reshape(row_count, model_width)
    normed_mid = rms_scale(own_rows.astype(jnp.float32), ffn_gain).astype(jnp.bfloat16)
    shared_gate_out = jnp.einsum(
        "td,fd->tf", normed_mid, shared_gate, preferred_element_type=jnp.float32
    )
    shared_up_out = jnp.einsum(
        "td,fd->tf", normed_mid, shared_up, preferred_element_type=jnp.float32
    )
    shared_act = (jax.nn.silu(shared_gate_out) * shared_up_out).astype(jnp.bfloat16)
    shared_part = jnp.dot(shared_act, shared_down, preferred_element_type=jnp.float32)
    summand = combine(place_back, group_part, shared_part, tp_count)
    output_share = scatter_all(summand).astype(jnp.float32)
    layer_out = (hidden_mine + output_share).astype(jnp.bfloat16)
    page_count = row_count // PAGE
    new_pages = cache_rows.reshape(page_count, PAGE, cache_rows.shape[1])
    cache_out = cache_pool.at[page_table[0, :page_count]].set(new_pages)
    return (layer_out, cache_out)


def solution(mesh):
    in_specs = (
        P("seq", "tp"),
        P("seq", None),
        P("seq", None),
        P("seq", None),
        P("seq", None, "tp"),
        P(),
        P(None, "tp"),
        P(None, "tp"),
        P("tp", None),
        P(),
        P(),
        P("seq", "tp", None),
        P("seq", "tp", None),
        P("seq", "tp", None),
        P("tp", None),
        P("tp", None),
        P("tp", None),
    )
    out_specs = (P("seq", "tp"), P("seq", None, "tp"))
    return jax.shard_map(shards, mesh=mesh, in_specs=in_specs, out_specs=out_specs, check_vma=False)
```

```python
import jax
import jax.numpy as jnp
from jax import lax
from jax.experimental import pallas as pl
from jax.experimental.pallas import tpu as pltpu
from jax.sharding import PartitionSpec as P

HEAD = 128
PAGE = 16


norm_eps = 1e-05
rope_base = 500000.0


def partner(block, axis, distance):
    count = lax.axis_size(axis)
    route = []
    for low in range(count):
        high = low | 1 << distance
        if high != low and high < count:
            route += [(low, high), (high, low)]
    return lax.ppermute(block, axis, route)


def gather_all(block):
    return lax.all_gather(block, ("seq", "tp"), axis=0)


def scatter_all(whole):
    part = lax.psum_scatter(whole, "tp", scatter_dimension=0, tiled=False)
    return lax.psum_scatter(part, "seq", scatter_dimension=0, tiled=False)


def dispatch_body(rows_ref, select_ref, gain_ref, router_ref, slot_ref, logit_ref):
    parts, _, width = rows_ref.shape
    total = None
    for part in range(parts):
        block = rows_ref[part].astype(jnp.float32)
        square = jnp.sum(block * block, axis=1, keepdims=True)
        total = square if total is None else total + square
    scale = lax.rsqrt(total / (parts * width) + norm_eps)
    select = select_ref[...]
    logit = None
    for part in range(parts):
        columns = slice(part * width, (part + 1) * width)
        normed = (
            rows_ref[part].astype(jnp.float32) * scale * gain_ref[:, columns]
        ).astype(jnp.bfloat16)
        slot_ref[:, columns] = jnp.dot(
            select, normed, preferred_element_type=jnp.float32
        ).astype(jnp.bfloat16)
        term = jnp.dot(normed, router_ref[columns, :], preferred_element_type=jnp.float32)
        logit = term if logit is None else logit + term
    logit_ref[...] = logit


def dispatch(gathered, select, gain, router):
    workers, parts, rows, width = gathered.shape
    slots = select.shape[1]
    model_width = parts * width
    return pl.pallas_call(
        dispatch_body,
        grid=(workers,),
        in_specs=[
            pl.BlockSpec((None, parts, rows, width), lambda w: (w, 0, 0, 0)),
            pl.BlockSpec((None, slots, rows), lambda w: (w, 0, 0)),
            pl.BlockSpec((1, model_width), lambda w: (0, 0)),
            pl.BlockSpec((model_width, router.shape[1]), lambda w: (0, 0)),
        ],
        out_specs=[
            pl.BlockSpec((None, slots, model_width), lambda w: (w, 0, 0)),
            pl.BlockSpec((None, rows, router.shape[1]), lambda w: (w, 0, 0)),
        ],
        out_shape=[
            jax.ShapeDtypeStruct((workers, slots, model_width), jnp.bfloat16),
            jax.ShapeDtypeStruct((workers, rows, router.shape[1]), jnp.float32),
        ],
        compiler_params=pltpu.CompilerParams(vmem_limit_bytes=32 << 20),
    )(gathered, select, gain[None, :], router)


def combine_body(parts, place_ref, expert_ref, shared_ref, out_ref):
    width = out_ref.shape[2]
    place = place_ref[...]
    is_mine = pl.program_id(0) == lax.axis_index("seq")
    for part in range(parts):
        columns = slice(part * width, (part + 1) * width)
        routed = jnp.dot(place, expert_ref[:, columns], preferred_element_type=jnp.float32)
        out_ref[part] = (routed + jnp.where(is_mine, shared_ref[:, columns], 0.0)).astype(
            jnp.bfloat16
        )


def combine(place, expert_rows, shared_part, parts):
    workers, rows, slots = place.shape
    model_width = expert_rows.shape[2]
    width = model_width // parts
    return pl.pallas_call(
        lambda *refs: combine_body(parts, *refs),
        grid=(workers,),
        in_specs=[
            pl.BlockSpec((None, rows, slots), lambda w: (w, 0, 0)),
            pl.BlockSpec((None, slots, model_width), lambda w: (w, 0, 0)),
            pl.BlockSpec((rows, model_width), lambda w: (0, 0)),
        ],
        out_specs=pl.BlockSpec((parts, None, rows, width), lambda w: (0, w, 0, 0)),
        out_shape=jax.ShapeDtypeStruct((parts, workers, rows, width), jnp.bfloat16),
        compiler_params=pltpu.CompilerParams(vmem_limit_bytes=32 << 20),
    )(place, expert_rows, shared_part)


def rms_scale(inputs, gain_vec):
    return (
        inputs * lax.rsqrt(jnp.mean(inputs * inputs, axis=-1, keepdims=True) + norm_eps) * gain_vec
    )


def in_segment(segment_row):
    row_order = jnp.arange(segment_row.shape[0], dtype=jnp.int32)
    before = (segment_row[:, None] == segment_row[None, :]) & (
        row_order[None, :] < row_order[:, None]
    )
    return jnp.sum(before.astype(jnp.int32), axis=1)


def rotate(inputs, position):
    half_size = inputs.shape[-1] // 2
    inv_freq = rope_base ** (-jnp.arange(half_size, dtype=jnp.float32) * 2.0 / inputs.shape[-1])
    angles = position.astype(jnp.float32)[:, None] * inv_freq[None, :]
    cosine = jnp.cos(angles)[:, None, :]
    sine_term = jnp.sin(angles)[:, None, :]
    leading = inputs[..., :half_size]
    trailing = inputs[..., half_size:]
    return jnp.concatenate(
        [leading * cosine - trailing * sine_term, trailing * cosine + leading * sine_term], axis=-1
    )


def shards(
    tokens,
    segments,
    routes,
    page_table,
    cache_pool,
    attn_gain,
    w_query,
    w_keyval,
    w_out,
    ffn_gain,
    w_router,
    expert_gate,
    expert_up,
    expert_down,
    shared_gate,
    shared_up,
    shared_down,
):
    tp_count = lax.axis_size("tp")
    seq_count = lax.axis_size("seq")
    tp_rank = lax.axis_index("tp")
    row_count = tokens.shape[0]
    col_width = tokens.shape[1]
    model_width = col_width * tp_count
    whole_rows = lax.all_gather(tokens, "tp", axis=1, tiled=True)
    residual = whole_rows.astype(jnp.float32)
    normed_in = rms_scale(residual, attn_gain).astype(jnp.bfloat16)
    segment_row = segments[0]
    position = in_segment(segment_row)
    local_heads = w_query.shape[1] // HEAD
    queries = jnp.dot(normed_in, w_query, preferred_element_type=jnp.float32).reshape(
        row_count, local_heads, HEAD
    )
    queries = rotate(queries, position).astype(jnp.bfloat16)
    keyval = jnp.dot(normed_in, w_keyval, preferred_element_type=jnp.float32)
    if w_keyval.shape[1] == HEAD:
        is_key = tp_rank % 2 == 0
        rotated = rotate(keyval.reshape(row_count, 1, HEAD), position).reshape(row_count, HEAD)
        own_half = jnp.where(is_key, rotated, keyval).astype(jnp.bfloat16)
        other_half = partner(own_half, "tp", 0)
        key_rows = jnp.where(is_key, own_half, other_half)
        values = jnp.where(is_key, other_half, own_half)
        cache_rows = own_half
    else:
        key_rows = (
            rotate(keyval[:, :HEAD].reshape(row_count, 1, HEAD), position)
            .reshape(row_count, HEAD)
            .astype(jnp.bfloat16)
        )
        values = keyval[:, HEAD:].astype(jnp.bfloat16)
        cache_rows = jnp.concatenate([key_rows, values], axis=1)
    scores = jnp.einsum(
        "qhd,kd->hqk", queries, key_rows, preferred_element_type=jnp.float32
    ) * HEAD ** (-0.5)
    row_order = jnp.arange(row_count, dtype=jnp.int32)
    allowed = (segment_row[:, None] == segment_row[None, :]) & (
        row_order[None, :] <= row_order[:, None]
    )
    weights = jnp.where(allowed[None], jnp.exp(scores), 0.0)
    attn_probs = (weights / jnp.sum(weights, axis=-1, keepdims=True)).astype(jnp.bfloat16)
    attended = jnp.einsum("hqk,kd->qhd", attn_probs, values, preferred_element_type=jnp.float32)
    attended = attended.astype(jnp.bfloat16).reshape(row_count, local_heads * HEAD)
    attn_part = jnp.dot(attended, w_out, preferred_element_type=jnp.float32)
    attn_mine = lax.psum_scatter(
        attn_part.astype(jnp.bfloat16)
        .reshape(row_count, tp_count, col_width)
        .transpose(1, 0, 2),
        "tp",
        scatter_dimension=0,
        tiled=False,
    )
    hidden_mine = tokens.astype(jnp.float32) + attn_mine.astype(jnp.float32)
    seq_rank = lax.axis_index("seq")
    gathered = gather_all(hidden_mine.astype(jnp.bfloat16))
    gathered = gathered.reshape(seq_count, tp_count, row_count, col_width)

    top_count = routes.shape[1]
    local_experts = expert_gate.shape[0]
    expert_total = local_experts * seq_count
    capacity = (
        (row_count * top_count * 5 // (expert_total * 3) + tp_count - 1) // tp_count * tp_count
    )
    capacity = (capacity + 15) // 16 * 16
    slots = local_experts * capacity
    marks = jnp.sum(
        (routes[:, :, None] == jnp.arange(expert_total, dtype=jnp.int32)).astype(jnp.float32),
        axis=1,
    ).astype(jnp.bfloat16)
    marks = jnp.pad(marks, ((0, 0), (0, -expert_total % 128)))
    shifted = [marks]
    for shift in range(1, seq_count):
        shifted.append(
            lax.ppermute(marks, "seq", [(i, (i + shift) % seq_count) for i in range(seq_count)])
        )
    turn = (seq_rank - jnp.arange(seq_count, dtype=jnp.int32)) % seq_count
    chosen = jnp.stack(shifted)[turn][:, :, :expert_total].astype(jnp.float32)
    first = seq_rank * local_experts
    named = lax.dynamic_slice_in_dim(chosen, first, local_experts, 2)
    earlier = (row_order[:, None] > row_order[None, :]).astype(jnp.bfloat16)
    rank = jnp.einsum(
        "ts,wse->wte", earlier, named.astype(jnp.bfloat16), preferred_element_type=jnp.float32
    ).astype(jnp.int32)
    place = jnp.where(named > 0, rank, -1)
    hit = place.transpose(0, 2, 1)[:, :, None, :] == jnp.arange(capacity, dtype=jnp.int32)[
        None, None, :, None
    ]
    select = hit.astype(jnp.bfloat16).reshape(seq_count, slots, row_count)
    place_back = (
        place[:, :, :, None] == jnp.arange(capacity, dtype=jnp.int32)[None, None, None, :]
    ).astype(jnp.bfloat16).reshape(seq_count, row_count, slots)
    slot_rows, logits = dispatch(gathered, select, ffn_gain, w_router)
    slot_rows = slot_rows.reshape(seq_count, local_experts, capacity, model_width)
    lifted = jnp.where(chosen > 0, jnp.exp(logits), 0.0)
    route_weight = lifted / jnp.sum(lifted, axis=2, keepdims=True)
    weight_mine = lax.dynamic_slice_in_dim(route_weight, first, local_experts, 2)
    slot_weight = jnp.sum(
        jnp.where(hit, weight_mine.transpose(0, 2, 1)[:, :, None, :], 0.0), axis=3
    )
    gate_out = jnp.einsum(
        "secd,efd->secf", slot_rows, expert_gate, preferred_element_type=jnp.float32
    )
    up_out = jnp.einsum("secd,efd->secf", slot_rows, expert_up, preferred_element_type=jnp.float32)
    activation = (jax.nn.silu(gate_out) * up_out * slot_weight[..., None]).astype(jnp.bfloat16)
    group_part = jnp.einsum(
        "secf,efd->secd", activation, expert_down, preferred_element_type=jnp.float32
    ).astype(jnp.bfloat16).reshape(seq_count, slots, model_width)
    own_rows = lax.dynamic_index_in_dim(gathered, seq_rank, 0, keepdims=False)
    own_rows = own_rows.transpose(1, 0, 2).reshape(row_count, model_width)
    normed_mid = rms_scale(own_rows.astype(jnp.float32), ffn_gain).astype(jnp.bfloat16)
    shared_gate_out = jnp.einsum(
        "td,fd->tf", normed_mid, shared_gate, preferred_element_type=jnp.float32
    )
    shared_up_out = jnp.einsum(
        "td,fd->tf", normed_mid, shared_up, preferred_element_type=jnp.float32
    )
    shared_act = (jax.nn.silu(shared_gate_out) * shared_up_out).astype(jnp.bfloat16)
    shared_part = jnp.dot(shared_act, shared_down, preferred_element_type=jnp.float32)
    summand = combine(place_back, group_part, shared_part, tp_count)
    output_share = scatter_all(summand).astype(jnp.float32)
    layer_out = (hidden_mine + output_share).astype(jnp.bfloat16)
    page_count = row_count // PAGE
    new_pages = cache_rows.reshape(page_count, PAGE, cache_rows.shape[1])
    cache_out = cache_pool.at[page_table[0, :page_count]].set(new_pages)
    return (layer_out, cache_out)


def solution(mesh):
    in_specs = (
        P("seq", "tp"),
        P("seq", None),
        P("seq", None),
        P("seq", None),
        P("seq", None, "tp"),
        P(),
        P(None, "tp"),
        P(None, "tp"),
        P("tp", None),
        P(),
        P(),
        P("seq", "tp", None),
        P("seq", "tp", None),
        P("seq", "tp", None),
        P("tp", None),
        P("tp", None),
        P("tp", None),
    )
    out_specs = (P("seq", "tp"), P("seq", None, "tp"))
    return jax.shard_map(shards, mesh=mesh, in_specs=in_specs, out_specs=out_specs, check_vma=False)
```
